1024 devices in a mesh: ctx: 32 (over z_lo, core), head: 4 (over x), seq: 8 (over y, z_hi).
Axes of the slice: x: 4, y: 4, z: 32 (z_hi: 2, z_lo: 16; z = z_hi * 16 + z_lo), core: 2. Of those that a mesh axis runs over, the one named last changes fastest.
Arguments:
- queries: bfloat16 [32768, 64, 128], P(('seq', 'ctx'), 'head'), parts along dimension 0, may hold values from -100 to 100
- keys: bfloat16 [32768, 4, 128], P(('seq', 'ctx'), 'head'), parts along dimension 0, may hold values from -8 to 8
- values: bfloat16 [32768, 4, 128], P(('seq', 'ctx'), 'head'), parts along dimension 0, may hold values from -6 to 6
Outputs:
- attended: bfloat16 [32768, 64, 128], P(('seq', 'ctx'), 'head'), parts along dimension 0
The draws below stay inside these ranges and needn't reach their ends.
There are 8 independent parts, one for each index of `seq`. The reference program is written for one: setup_inputs(seed, part) draws one part's arguments, and reference() takes and returns one part's arrays. A program takes and returns all parts, laid end to end along the dimension named above; each array names one. Nothing has to cross between parts.
All inputs are finite; a program needn't handle non-finite values.
Results may differ from the reference program's by a relative error of at most 0.0035.
Values may be sent and summed in bfloat16 or wider, within the bound.
A program may use at most 32 MiB of HBM per device.

```python
import math
import jax
import jax.numpy as jnp
from jax import lax

HD = 128
GROUP = 16
KVH = 4
HQ = 64
SEQ_LEN = 4096


def common_pair(key):
    base = jax.random.fold_in(key, 7)
    first, second = jax.random.split(base, 2)
    query_draw = 2.5 * jax.random.truncated_normal(first, -6.0, 6.0, (SEQ_LEN, HQ, HD), jnp.float32)
    key_draw = jax.random.truncated_normal(second, -6.0, 6.0, (SEQ_LEN, KVH, HD), jnp.float32)
    return (query_draw, key_draw)


def draw_queries(key, part):
    return common_pair(key)[0].astype(jnp.bfloat16)


def draw_keys(key, part):
    return common_pair(key)[1].astype(jnp.bfloat16)


def level_of(stream_key, dims, cuts, low, top_value):
    def one(axis_at, shards_of):
        steps = jax.random.uniform(jax.random.fold_in(jax.random.fold_in(stream_key, 6), axis_at), (shards_of,), jnp.float32, low / len(cuts), top_value / len(cuts))
        return jnp.repeat(jnp.exp(steps), dims[axis_at] // shards_of).reshape((-1,) + (1,) * (len(dims) - axis_at - 1))

    level = one(*cuts[0])
    for cut in cuts[1:]:
        level = level * one(*cut)
    return level


def gaussian(key, extent, deviation, most, cuts=(), kind=jnp.bfloat16):
    entries = jax.random.normal(key, extent, jnp.float32) * deviation
    if len(cuts) > 0:
        entries = level_of(key, extent, cuts, -0.22, 0.18) * entries
    return jnp.clip(entries, min=-most, max=most).astype(kind)


def setup_inputs(seed: int = 0, part: int = 0) -> dict:
    streams_of = jax.random.split(jax.random.key(seed), 4)
    own_keys = jax.random.split(jax.random.fold_in(streams_of[3], part), 4)
    queries = draw_queries(jax.random.fold_in(jax.random.fold_in(streams_of[3], part), 71), part)
    keys = draw_keys(jax.random.fold_in(jax.random.fold_in(streams_of[3], part), 71), part)
    values = gaussian(own_keys[2], (SEQ_LEN, KVH, HD), 1.0, 6.0, ((0, 32), (1, 4)))
    return {"queries": queries, "keys": keys, "values": values}


def reference(queries, keys, values):
    seq_total = queries.shape[0]
    block_rows = math.gcd(seq_total, 512)
    scale = 1.0 / math.sqrt(HD)
    key_places = jnp.arange(seq_total, dtype=jnp.int32)
    pieces_out = []
    for head_group in range(KVH):
        key_group = keys[:, head_group, :].astype(jnp.float32)
        value_group = values[:, head_group, :].astype(jnp.float32)
        query_group = queries[:, head_group * GROUP:(head_group + 1) * GROUP, :]
        query_group = query_group.reshape(seq_total // block_rows, block_rows, GROUP, HD)
        firsts = jnp.arange(seq_total // block_rows, dtype=jnp.int32) * block_rows

        def one_block(item):
            query_block, first_row = item
            scores = jnp.einsum('rhd,nd->rhn', query_block.astype(jnp.float32), key_group) * scale
            query_places = first_row + jnp.arange(block_rows, dtype=jnp.int32)
            visible = key_places[None, None, :] <= query_places[:, None, None]
            scores = jnp.where(visible, scores, -1e+30)
            top = lax.optimization_barrier(jnp.max(scores, axis=-1, keepdims=True))
            expo = jnp.where(visible, jnp.exp(scores - top), 0.0)
            total = lax.optimization_barrier(jnp.sum(expo, axis=-1))
            weights = expo.astype(jnp.bfloat16).astype(jnp.float32)
            numer = jnp.einsum('rhn,nd->rhd', weights, value_group)
            return (numer / total[..., None]).astype(jnp.bfloat16)
        result = lax.map(one_block, (query_group, firsts))
        pieces_out.append(result.reshape(seq_total, GROUP, HD))
    return jnp.concatenate(pieces_out, axis=1)
```

```python
import functools
import math

import jax
import jax.numpy as jnp
from jax import lax
from jax.experimental import pallas as pl
from jax.experimental.pallas import tpu as pltpu
from jax.sharding import PartitionSpec as P

MESH = pl.DeviceIdType.MESH
TILE = 256
PIECES = 2
HALVES = 1
TABLE = (
    (416,),
    (545, 0),
    (674, 160, 1),
    (803, 9024, 289, 2),
    (932, 13249, 418, 3, 0),
    (1061, 17474, 547, 4, 544, 1),
    (1190, 21699, 676, 5, 21696, 673, 2),
    (1319, 25924, 805, 6, 25921, 802, 3, 0),
    (1448, 30149, 934, 7, 30146, 931, 4, 928, 1),
    (1577, 34374, 1063, 8, 34371, 1060, 34368, 5, 1057, 2),
    (1706, 38599, 1192, 9, 38596, 1189, 38593, 6, 1186, 3, 0),
    (1835, 42824, 1321, 10, 42821, 1318, 42818, 7, 1315, 4, 1312, 1),
    (1708, 46793, 1450, 11, 46790, 1447, 8, 46787, 1444, 46784, 5, 1441, 2),
    (1837, 1836, 51018, 1579, 1833, 51015, 1576, 1830, 51012, 1573, 1827, 51009, 1824, 1570),
    (1966, 1965, 55243, 1964, 1962, 55240, 1961, 1959, 55237, 1958, 1956, 55234, 1955, 1953, 1952),
    (15, 14, 13, 11, 12, 10, 8, 9, 7, 5, 6, 4, 2, 3, 1, 0),
)


def unpack(item):
    targets = [item // 128 // 32**i % 32 for i in range(item // 32 % 4)]
    return item % 16, item // 16 % 2, [(t % 16, t // 16) for t in targets]


def kernel(
    chips, group, q_hbm, k_hbm, v_hbm, o_ref,
    q_ref, k_ref, v_ref, m_ref, l_ref, acc_ref,
    load_sem, recv_sem, pair_sem, send_sem,
):
    me = lax.axis_index("ctx")
    seq = lax.axis_index("seq")
    chip, core = me // 2, me % 2
    rows = k_hbm.shape[0]
    piece_rows = rows // PIECES
    total_rows = q_ref.shape[0]
    factor = math.log2(math.e) / math.sqrt(q_ref.shape[1])

    def device(chip_at, core_at, other=0):
        return {"ctx": chip_at * 2 + core_at, "seq": seq + other * (1 - 2 * (seq % 2))}

    def rows_of(ref, slot, piece=None):
        start = slot * rows
        if piece is None:
            return ref.at[pl.ds(pl.multiple_of(start, rows), rows)]
        return ref.at[pl.ds(pl.multiple_of(start + piece * piece_rows, piece_rows), piece_rows)]

    loads = [
        pltpu.make_async_copy(k_hbm, rows_of(k_ref, me), load_sem.at[0]),
        pltpu.make_async_copy(v_hbm, rows_of(v_ref, me), load_sem.at[1]),
        pltpu.make_async_copy(q_hbm, q_ref, load_sem.at[2]),
    ]
    for load in loads:
        load.start()

    def pick(values):
        out = jnp.int32(values[0])
        for c in range(1, chips):
            if values[c] != values[0]:
                out = jnp.where(chip == c, values[c], out)
        return out

    senders = [set() for _ in range(chips)]
    receivers = [set() for _ in range(chips)]
    for c in range(chips):
        for item in TABLE[c]:
            for target, other in unpack(item)[2]:
                receivers[c].add((target, other))
                senders[target].add((c, other))
    barrier = pltpu.get_barrier_semaphore()
    for other in (1, 0):
        for c in range(chips):
            flags = [int((c, other) in senders[t]) for t in range(chips)]
            if any(flags):

                @pl.when(pick(flags) == 1)
                def _():
                    pl.semaphore_signal(barrier, inc=1, device_id=device(c, core, other), device_id_type=MESH)

    pl.semaphore_signal(barrier, inc=1, device_id=device(chip, 1 - core), device_id_type=MESH)
    longest = max(len(row) for row in TABLE)
    row = [pick([row[n] if n < len(row) else 0 for row in TABLE]) for n in range(longest)]

    def item_of(n):
        out = row[0]
        for i in range(1, longest):
            out = jnp.where(n == i, row[i], out)
        return out

    item_count = pick([len(row) for row in TABLE])
    for load in loads[:2]:
        load.wait()
    pl.semaphore_wait(barrier, 1 + pick([len(r) for r in receivers]))

    refs = (k_ref, v_ref)
    parts = [(kind, piece) for kind in range(2) for piece in range(PIECES)]
    degree = max(item // 32 % 4 for row in TABLE for item in row)

    def remote(here, there, n, arrived, target):
        return pltpu.make_async_remote_copy(
            src_ref=here, dst_ref=there, send_sem=send_sem.at[n], recv_sem=arrived,
            device_id=target, device_id_type=MESH,
        )

    def at_home(s):
        return 2 * s + core

    def away(s):
        return 2 * chips + s

    def send_on(n, item, kind, piece):
        s, foreign = item % 16, item // 16 % 2
        count = item // 32 % 4
        ref = refs[kind]
        here = rows_of(ref, jnp.where(foreign == 1, away(s), at_home(s)), piece)
        for i in range(degree):
            target = item // (128 * 32**i) % 32
            other = target // 16
            lands = jnp.logical_and(other == 1, foreign == 0)
            copy = remote(
                here,
                rows_of(ref, jnp.where(lands, away(s), at_home(s)), piece),
                n,
                recv_sem.at[jnp.where(lands, chips + s, s), kind, piece],
                device(target % 16, core, other),
            )
            pl.when(i < count)(copy.start)

    def across(n, s, kind):
        block = rows_of(refs[kind], at_home(s))
        return remote(block, block, n, pair_sem.at[s, kind], device(chip, 1 - core))

    def relay(n, item, kind):
        s, foreign = item % 16, item // 16 % 2
        for piece in range(PIECES):
            block = rows_of(refs[kind], jnp.where(foreign == 1, away(s), at_home(s)), piece)
            arrived = recv_sem.at[jnp.where(foreign == 1, chips + s, s), kind, piece]
            remote(block, block, n, arrived, device(chip, 1 - core)).wait_recv()
            send_on(n, item, kind, piece)
        pl.when(foreign == 0)(across(n, s, kind).start)

    def paired(s):
        for kind in range(2):
            block = rows_of(refs[kind], 2 * s + 1 - core)
            remote(block, block, 0, pair_sem.at[s, kind], device(chip, 1 - core)).wait_recv()

    def sent(n):
        item = item_of(n)
        count = item // 32 % 4 + 1 - item // 16 % 2
        for times in range(1, degree + 2):

            @pl.when(count == times)
            def _():
                bulk = k_ref.at[pl.ds(0, times * 2 * rows)]
                remote(bulk, bulk, n, pair_sem.at[0, 0], device(chip, 1 - core)).wait_send()

    for kind in range(2):
        for piece in range(PIECES):
            send_on(0, row[0], kind, piece)
        across(0, chip, kind).start()
    loads[2].wait()

    wide = 2 * rows
    tiles = total_rows // TILE

    def first(tile):
        at = pl.ds(tile * TILE, TILE)
        keys = pl.ds(pl.multiple_of(chip * wide, wide), wide)
        s = lax.dot_general(
            q_ref[at], k_ref[keys], (((1,), (1,)), ((), ())), preferred_element_type=jnp.float32
        )
        place = core * rows + (tile * TILE + lax.broadcasted_iota(jnp.int32, s.shape, 0)) // group
        s = jnp.where(lax.broadcasted_iota(jnp.int32, s.shape, 1) <= place, s, -1e30)
        top = jnp.max(s, axis=1, keepdims=True)
        p = jnp.exp2((s - top) * factor)
        m_ref[at] = jnp.broadcast_to(top, (TILE, 128))
        part = p[:, :128]
        for j in range(128, wide, 128):
            part += p[:, j : j + 128]
        l_ref[at] = part
        acc_ref[at] = jnp.dot(p.astype(jnp.bfloat16), v_ref[keys], preferred_element_type=jnp.float32)

    def absorb(tile, s_chip):
        at = pl.ds(tile * TILE, TILE)
        keys = pl.ds(pl.multiple_of(s_chip * wide, wide), wide)
        s = lax.dot_general(
            q_ref[at], k_ref[keys], (((1,), (1,)), ((), ())), preferred_element_type=jnp.float32
        )
        old = m_ref[at]
        top = jnp.maximum(old, jnp.max(s, axis=1, keepdims=True))
        shrink = jnp.exp2((old - top) * factor)
        m_ref[at] = top
        ps = []
        part = l_ref[at] * shrink
        for j in range(0, wide, 128):
            p = jnp.exp2((s[:, j : j + 128] - top) * factor)
            part += p
            ps.append(p.astype(jnp.bfloat16))
        l_ref[at] = part
        p = jnp.concatenate(ps, axis=1)
        acc_ref[at] = acc_ref[at] * shrink + jnp.dot(
            p, v_ref[keys], preferred_element_type=jnp.float32
        )

    paired(chip)
    for tile in range(tiles):
        first(tile)

    def half(i, s):
        for tile in range(i * tiles // HALVES, (i + 1) * tiles // HALVES):
            absorb(tile, s)

    def step(n, waiting):
        item = item_of(n)
        fresh = item // 16 % 2 == 0
        ready = jnp.logical_and(fresh, waiting >= 0)
        for kind in range(2):
            relay(n, item, kind)
            if HALVES == 2 or kind == 1:

                @pl.when(ready)
                def _():
                    if kind == HALVES % 2:
                        paired(waiting)
                    half(kind if HALVES == 2 else 0, waiting)

        return jnp.where(fresh, item % 16, waiting)

    waiting = lax.fori_loop(1, item_count, step, jnp.int32(-1))

    @pl.when(waiting >= 0)
    def _():
        paired(waiting)
        for i in range(HALVES):
            half(i, waiting)

    for tile in range(tiles):
        at = pl.ds(tile * TILE, TILE)
        total = jnp.sum(l_ref[at], axis=1, keepdims=True)
        o_ref[at] = (acc_ref[at] * (1.0 / total)).astype(o_ref.dtype)

    def finish(n, carry):
        sent(n)
        return carry

    lax.fori_loop(0, item_count, finish, 0)


def attend(ctx, queries, keys, values):
    count, heads, width = queries.shape
    group = heads // keys.shape[1]
    rows = count * group
    q = queries.reshape(rows, width)
    k = keys.reshape(count, width)
    v = values.reshape(count, width)
    chips = ctx // 2
    longest = max(len(row) for row in TABLE)
    far = [item % 16 for row in TABLE for item in row if item // 16 % 2]
    slots = ctx + max(far, default=-1) + 1
    anywhere = pl.BlockSpec(memory_space=pltpu.HBM)
    out = pl.pallas_call(
        functools.partial(kernel, chips, group),
        out_shape=jax.ShapeDtypeStruct((rows, width), queries.dtype),
        in_specs=[anywhere] * 3,
        out_specs=pl.BlockSpec(memory_space=pltpu.VMEM),
        scratch_shapes=[
            pltpu.VMEM((rows, width), queries.dtype),
            pltpu.VMEM((slots * count, width), keys.dtype),
            pltpu.VMEM((slots * count, width), values.dtype),
            pltpu.VMEM((rows, 128), jnp.float32),
            pltpu.VMEM((rows, 128), jnp.float32),
            pltpu.VMEM((rows, width), jnp.float32),
            pltpu.SemaphoreType.DMA((3,)),
            pltpu.SemaphoreType.DMA((slots - chips, 2, PIECES)),
            pltpu.SemaphoreType.DMA((chips, 2)),
            pltpu.SemaphoreType.DMA((longest,)),
        ],
        compiler_params=pltpu.CompilerParams(
            collective_id=0, has_side_effects=True, vmem_limit_bytes=32 * 1024 * 1024
        ),
        name="attend",
    )(*(pltpu.with_memory_space_constraint(a, pltpu.HBM) for a in (q, k, v)))
    return out.reshape(count, heads, width)


def solution(mesh):
    spec = P(("seq", "ctx"), "head", None)
    return jax.shard_map(
        functools.partial(attend, mesh.shape["ctx"]),
        mesh=mesh,
        in_specs=(spec, spec, spec),
        out_specs=spec,
        check_vma=False,
    )
```

```python
import functools
import math

import jax
import jax.numpy as jnp
from jax import lax
from jax.experimental import pallas as pl
from jax.experimental.pallas import tpu as pltpu
from jax.sharding import PartitionSpec as P

MESH = pl.DeviceIdType.MESH
TILE = 512
PIECES = 1
LATE = 5
HALVES = 1
TABLE = (
    (416,),
    (545, 0),
    (674, 0, 1),
    (803, 140128, 1, 2),
    (932, 275425, 2, 3, 0),
    (1061, 410722, 3, 4, 0, 1),
    (1190, 546019, 4, 546016, 5, 1, 2),
    (1319, 681316, 5, 681313, 6, 2, 3, 0),
    (1448, 816613, 6, 816610, 7, 3, 4, 0, 1),
    (1577, 951910, 7, 951907, 8, 4, 951904, 5, 1, 2),
    (1706, 1087207, 8, 1087204, 9, 5, 1087201, 6, 2, 3, 0),
    (1835, 1222504, 9, 1222501, 10, 6, 1222498, 7, 3, 4, 0, 1),
    (1964, 1357801, 10, 1357798, 11, 1357795, 7, 8, 1357792, 4, 5, 1, 2),
    (1837, 1492842, 11, 12, 1492839, 8, 9, 1492836, 5, 1492833, 6, 2, 3, 0),
    (1966, 1965, 1628139, 12, 1962, 1628136, 9, 1959, 1628133, 6, 1956, 1628130, 3, 1953, 0),
    (15, 14, 55116, 13, 11, 55113, 10, 8, 55110, 7, 5, 55107, 4, 55104, 2, 1),
)


def unpack(item):
    targets = [item // 128 // 32**i % 32 for i in range(item // 32 % 4)]
    return item % 16, item // 16 % 2, [(t % 16, t // 16) for t in targets]


def kernel(
    chips, group, q_hbm, k_hbm, v_hbm, o_ref,
    q_ref, k_ref, v_ref, m_ref, l_ref, acc_ref,
    load_sem, recv_sem, pair_sem, send_sem,
):
    me = lax.axis_index("ctx")
    seq = lax.axis_index("seq")
    chip, core = me // 2, me % 2
    rows = k_hbm.shape[0]
    piece_rows = rows // PIECES
    total_rows = q_ref.shape[0]
    factor = math.log2(math.e) / math.sqrt(q_ref.shape[1])

    def device(chip_at, core_at, other=0):
        return {"ctx": chip_at * 2 + core_at, "seq": seq + other * (1 - 2 * (seq % 2))}

    def rows_of(ref, slot, piece=None):
        start = slot * rows
        if piece is None:
            return ref.at[pl.ds(pl.multiple_of(start, rows), rows)]
        return ref.at[pl.ds(pl.multiple_of(start + piece * piece_rows, piece_rows), piece_rows)]

    loads = [
        pltpu.make_async_copy(k_hbm, rows_of(k_ref, me), load_sem.at[0]),
        pltpu.make_async_copy(v_hbm, rows_of(v_ref, me), load_sem.at[1]),
        pltpu.make_async_copy(q_hbm, q_ref, load_sem.at[2]),
    ]
    for load in loads:
        load.start()

    def pick(values):
        out = jnp.int32(values[0])
        for c in range(1, chips):
            if values[c] != values[0]:
                out = jnp.where(chip == c, values[c], out)
        return out

    senders = [set() for _ in range(chips)]
    receivers = [set() for _ in range(chips)]
    for c in range(chips):
        for item in TABLE[c]:
            for target, other in unpack(item)[2]:
                receivers[c].add((target, other))
                senders[target].add((c, other))
    barrier = pltpu.get_barrier_semaphore()
    for other in (1, 0):
        for c in range(chips):
            flags = [int((c, other) in senders[t]) for t in range(chips)]
            if any(flags):

                @pl.when(pick(flags) == 1)
                def _():
                    pl.semaphore_signal(barrier, inc=1, device_id=device(c, core, other), device_id_type=MESH)

    pl.semaphore_signal(barrier, inc=1, device_id=device(chip, 1 - core), device_id_type=MESH)
    longest = max(len(row) for row in TABLE)
    row = [pick([row[n] if n < len(row) else 0 for row in TABLE]) for n in range(longest)]

    def item_of(n):
        out = row[0]
        for i in range(1, longest):
            out = jnp.where(n == i, row[i], out)
        return out

    item_count = pick([len(row) for row in TABLE])
    for load in loads[:2]:
        load.wait()
    pl.semaphore_wait(barrier, 1 + pick([len(r) for r in receivers]))

    refs = (k_ref, v_ref)
    parts = [(kind, piece) for kind in range(2) for piece in range(PIECES)]
    degree = max(item // 32 % 4 for row in TABLE for item in row)

    def remote(here, there, n, arrived, target):
        return pltpu.make_async_remote_copy(
            src_ref=here, dst_ref=there, send_sem=send_sem.at[n], recv_sem=arrived,
            device_id=target, device_id_type=MESH,
        )

    def at_home(s):
        return 2 * s + core

    def away(s):
        return 2 * chips + s

    def send_on(n, item, kind, piece):
        s, foreign = item % 16, item // 16 % 2
        count = item // 32 % 4
        ref = refs[kind]
        here = rows_of(ref, jnp.where(foreign == 1, away(s), at_home(s)), piece)
        for i in range(degree):
            target = item // (128 * 32**i) % 32
            other = target // 16
            lands = jnp.logical_and(other == 1, foreign == 0)
            copy = remote(
                here,
                rows_of(ref, jnp.where(lands, away(s), at_home(s)), piece),
                n,
                recv_sem.at[jnp.where(lands, chips + s, s), kind, piece],
                device(target % 16, core, other),
            )
            pl.when(i < count)(copy.start)

    def across(n, s, kind):
        block = rows_of(refs[kind], at_home(s))
        return remote(block, block, n, pair_sem.at[s, kind], device(chip, 1 - core))

    def relay(n, item, kind):
        s, foreign = item % 16, item // 16 % 2
        for piece in range(PIECES):
            block = rows_of(refs[kind], jnp.where(foreign == 1, away(s), at_home(s)), piece)
            arrived = recv_sem.at[jnp.where(foreign == 1, chips + s, s), kind, piece]
            remote(block, block, n, arrived, device(chip, 1 - core)).wait_recv()
            send_on(n, item, kind, piece)
        pl.when(foreign == 0)(across(n, s, kind).start)

    def paired(s):
        for kind in range(2):
            block = rows_of(refs[kind], 2 * s + 1 - core)
            remote(block, block, 0, pair_sem.at[s, kind], device(chip, 1 - core)).wait_recv()

    def sent(n):
        item = item_of(n)
        count = item // 32 % 4 + 1 - item // 16 % 2
        for times in range(1, degree + 2):

            @pl.when(count == times)
            def _():
                bulk = k_ref.at[pl.ds(0, times * 2 * rows)]
                remote(bulk, bulk, n, pair_sem.at[0, 0], device(chip, 1 - core)).wait_send()

    for kind in range(2):
        for piece in range(PIECES):
            send_on(0, row[0], kind, piece)
        across(0, chip, kind).start()
    loads[2].wait()

    wide = 2 * rows
    tiles = total_rows // TILE

    def first(tile):
        at = pl.ds(tile * TILE, TILE)
        keys = pl.ds(pl.multiple_of(chip * wide, wide), wide)
        s = lax.dot_general(
            q_ref[at], k_ref[keys], (((1,), (1,)), ((), ())), preferred_element_type=jnp.float32
        )
        place = core * rows + (tile * TILE + lax.broadcasted_iota(jnp.int32, s.shape, 0)) // group
        s = jnp.where(lax.broadcasted_iota(jnp.int32, s.shape, 1) <= place, s, -1e30)
        top = jnp.max(s, axis=1, keepdims=True)
        p = jnp.exp2((s - top) * factor)
        m_ref[at] = jnp.broadcast_to(top, (TILE, 128))
        part = p[:, :128]
        for j in range(128, wide, 128):
            part += p[:, j : j + 128]
        l_ref[at] = part
        acc_ref[at] = jnp.dot(p.astype(jnp.bfloat16), v_ref[keys], preferred_element_type=jnp.float32)

    def absorb(tile, s_chip):
        at = pl.ds(tile * TILE, TILE)
        keys = pl.ds(pl.multiple_of(s_chip * wide, wide), wide)
        s = lax.dot_general(
            q_ref[at], k_ref[keys], (((1,), (1,)), ((), ())), preferred_element_type=jnp.float32
        )
        old = m_ref[at]
        top = jnp.maximum(old, jnp.max(s, axis=1, keepdims=True))
        shrink = jnp.exp2((old - top) * factor)
        m_ref[at] = top
        ps = []
        part = l_ref[at] * shrink
        for j in range(0, wide, 128):
            p = jnp.exp2((s[:, j : j + 128] - top) * factor)
            part += p
            ps.append(p.astype(jnp.bfloat16))
        l_ref[at] = part
        p = jnp.concatenate(ps, axis=1)
        acc_ref[at] = acc_ref[at] * shrink + jnp.dot(
            p, v_ref[keys], preferred_element_type=jnp.float32
        )

    paired(chip)
    for tile in range(tiles):
        first(tile)

    def half(i, s):
        for tile in range(i * tiles // HALVES, (i + 1) * tiles // HALVES):
            absorb(tile, s)

    def step(n, waiting):
        item = item_of(n)
        fresh = item // 16 % 2 == 0
        pl.when(n >= LATE)(functools.partial(sent, n - LATE))
        ready = jnp.logical_and(fresh, waiting >= 0)
        for kind in range(2):
            relay(n, item, kind)
            if HALVES == 2 or kind == 1:

                @pl.when(ready)
                def _():
                    if kind == HALVES % 2:
                        paired(waiting)
                    half(kind if HALVES == 2 else 0, waiting)

        return jnp.where(fresh, item % 16, waiting)

    waiting = lax.fori_loop(1, item_count, step, jnp.int32(-1))

    @pl.when(waiting >= 0)
    def _():
        paired(waiting)
        for i in range(HALVES):
            half(i, waiting)

    for tile in range(tiles):
        at = pl.ds(tile * TILE, TILE)
        total = jnp.sum(l_ref[at], axis=1, keepdims=True)
        o_ref[at] = (acc_ref[at] * (1.0 / total)).astype(o_ref.dtype)

    def finish(n, carry):
        sent(n)
        return carry

    lax.fori_loop(jnp.maximum(item_count - LATE, 0), item_count, finish, 0)


def attend(ctx, queries, keys, values):
    count, heads, width = queries.shape
    group = heads // keys.shape[1]
    rows = count * group
    q = queries.reshape(rows, width)
    k = keys.reshape(count, width)
    v = values.reshape(count, width)
    chips = ctx // 2
    longest = max(len(row) for row in TABLE)
    far = [item % 16 for row in TABLE for item in row if item // 16 % 2]
    slots = ctx + max(far, default=-1) + 1
    anywhere = pl.BlockSpec(memory_space=pltpu.HBM)
    out = pl.pallas_call(
        functools.partial(kernel, chips, group),
        out_shape=jax.ShapeDtypeStruct((rows, width), queries.dtype),
        in_specs=[anywhere] * 3,
        out_specs=pl.BlockSpec(memory_space=pltpu.VMEM),
        scratch_shapes=[
            pltpu.VMEM((rows, width), queries.dtype),
            pltpu.VMEM((slots * count, width), keys.dtype),
            pltpu.VMEM((slots * count, width), values.dtype),
            pltpu.VMEM((rows, 128), jnp.float32),
            pltpu.VMEM((rows, 128), jnp.float32),
            pltpu.VMEM((rows, width), jnp.float32),
            pltpu.SemaphoreType.DMA((3,)),
            pltpu.SemaphoreType.DMA((slots - chips, 2, PIECES)),
            pltpu.SemaphoreType.DMA((chips, 2)),
            pltpu.SemaphoreType.DMA((longest,)),
        ],
        compiler_params=pltpu.CompilerParams(
            collective_id=0, has_side_effects=True, vmem_limit_bytes=32 * 1024 * 1024
        ),
        name="attend",
    )(*(pltpu.with_memory_space_constraint(a, pltpu.HBM) for a in (q, k, v)))
    return out.reshape(count, heads, width)


def solution(mesh):
    spec = P(("seq", "ctx"), "head", None)
    return jax.shard_map(
        functools.partial(attend, mesh.shape["ctx"]),
        mesh=mesh,
        in_specs=(spec, spec, spec),
        out_specs=spec,
        check_vma=False,
    )
```

```python
import functools
import math

import jax
import jax.numpy as jnp
from jax import lax
from jax.experimental import pallas as pl
from jax.experimental.pallas import tpu as pltpu
from jax.sharding import PartitionSpec as P

MESH = pl.DeviceIdType.MESH
TILE = 512
PIECES = 1
LATE = 5
HALVES = 1
TABLE = (
    (416,),
    (545, 0),
    (674, 0, 1),
    (803, 267104, 1, 2),
    (932, 402401, 2, 3, 0),
    (1061, 537698, 3, 4, 0, 1),
    (1190, 672995, 4, 672992, 5, 1, 2),
    (1319, 808292, 5, 808289, 6, 2, 3, 0),
    (1448, 943589, 6, 943586, 7, 3, 4, 0, 1),
    (1577, 1078886, 7, 1078883, 8, 4, 1078880, 5, 1, 2),
    (1706, 1214183, 8, 1214180, 9, 5, 1214177, 6, 2, 3, 0),
    (1835, 1349480, 9, 1349477, 10, 6, 1349474, 7, 3, 4, 0, 1),
    (1964, 1484777, 10, 1484774, 11, 1484771, 7, 8, 1484768, 4, 5, 1, 2),
    (1837, 1619818, 11, 12, 1619815, 8, 9, 1619812, 5, 1619809, 6, 2, 3, 0),
    (1966, 1965, 1755115, 12, 1962, 1755112, 9, 1959, 1755109, 6, 1956, 1755106, 3, 1953, 0),
    (15, 14, 59084, 13, 11, 59081, 10, 8, 59078, 7, 5, 59075, 4, 59072, 2, 1),
)


def unpack(item):
    targets = [item // 128 // 32**i % 32 for i in range(item // 32 % 4)]
    return item % 16, item // 16 % 2, [(t % 16, t // 16) for t in targets]


def kernel(
    chips, group, q_hbm, k_hbm, v_hbm, o_ref,
    q_ref, k_ref, v_ref, m_ref, l_ref, acc_ref,
    load_sem, recv_sem, pair_sem, send_sem,
):
    me = lax.axis_index("ctx")
    seq = lax.axis_index("seq")
    chip, core = me // 2, me % 2
    rows = k_hbm.shape[0]
    piece_rows = rows // PIECES
    total_rows = q_ref.shape[0]
    factor = math.log2(math.e) / math.sqrt(q_ref.shape[1])

    def device(chip_at, core_at, other=0):
        return {"ctx": chip_at * 2 + core_at, "seq": seq + other * (1 - 2 * (seq % 2))}

    def rows_of(ref, slot, piece=None):
        start = slot * rows
        if piece is None:
            return ref.at[pl.ds(pl.multiple_of(start, rows), rows)]
        return ref.at[pl.ds(pl.multiple_of(start + piece * piece_rows, piece_rows), piece_rows)]

    loads = [
        pltpu.make_async_copy(k_hbm, rows_of(k_ref, me), load_sem.at[0]),
        pltpu.make_async_copy(v_hbm, rows_of(v_ref, me), load_sem.at[1]),
        pltpu.make_async_copy(q_hbm, q_ref, load_sem.at[2]),
    ]
    for load in loads:
        load.start()

    def pick(values):
        out = jnp.int32(values[0])
        for c in range(1, chips):
            if values[c] != values[0]:
                out = jnp.where(chip == c, values[c], out)
        return out

    senders = [set() for _ in range(chips)]
    receivers = [set() for _ in range(chips)]
    for c in range(chips):
        for item in TABLE[c]:
            for target, other in unpack(item)[2]:
                receivers[c].add((target, other))
                senders[target].add((c, other))
    barrier = pltpu.get_barrier_semaphore()
    for other in (1, 0):
        for c in range(chips):
            flags = [int((c, other) in senders[t]) for t in range(chips)]
            if any(flags):

                @pl.when(pick(flags) == 1)
                def _():
                    pl.semaphore_signal(barrier, inc=1, device_id=device(c, core, other), device_id_type=MESH)

    pl.semaphore_signal(barrier, inc=1, device_id=device(chip, 1 - core), device_id_type=MESH)
    longest = max(len(row) for row in TABLE)
    row = [pick([row[n] if n < len(row) else 0 for row in TABLE]) for n in range(longest)]

    def item_of(n):
        out = row[0]
        for i in range(1, longest):
            out = jnp.where(n == i, row[i], out)
        return out

    item_count = pick([len(row) for row in TABLE])
    for load in loads[:2]:
        load.wait()
    pl.semaphore_wait(barrier, 1 + pick([len(r) for r in receivers]))

    refs = (k_ref, v_ref)
    parts = [(kind, piece) for kind in range(2) for piece in range(PIECES)]
    degree = max(item // 32 % 4 for row in TABLE for item in row)

    def remote(here, there, n, arrived, target):
        return pltpu.make_async_remote_copy(
            src_ref=here, dst_ref=there, send_sem=send_sem.at[n], recv_sem=arrived,
            device_id=target, device_id_type=MESH,
        )

    def at_home(s):
        return 2 * s + core

    def away(s):
        return 2 * chips + s

    def send_on(n, item, kind, piece):
        s, foreign = item % 16, item // 16 % 2
        count = item // 32 % 4
        ref = refs[kind]
        here = rows_of(ref, jnp.where(foreign == 1, away(s), at_home(s)), piece)
        for i in range(degree):
            target = item // (128 * 32**i) % 32
            other = target // 16
            lands = jnp.logical_and(other == 1, foreign == 0)
            copy = remote(
                here,
                rows_of(ref, jnp.where(lands, away(s), at_home(s)), piece),
                n,
                recv_sem.at[jnp.where(lands, chips + s, s), kind, piece],
                device(target % 16, core, other),
            )
            pl.when(i < count)(copy.start)

    def across(n, s, kind):
        block = rows_of(refs[kind], at_home(s))
        return remote(block, block, n, pair_sem.at[s, kind], device(chip, 1 - core))

    def relay(n, item, kind):
        s, foreign = item % 16, item // 16 % 2
        for piece in range(PIECES):
            block = rows_of(refs[kind], jnp.where(foreign == 1, away(s), at_home(s)), piece)
            arrived = recv_sem.at[jnp.where(foreign == 1, chips + s, s), kind, piece]
            remote(block, block, n, arrived, device(chip, 1 - core)).wait_recv()
            send_on(n, item, kind, piece)
        pl.when(foreign == 0)(across(n, s, kind).start)

    def paired(s):
        for kind in range(2):
            block = rows_of(refs[kind], 2 * s + 1 - core)
            remote(block, block, 0, pair_sem.at[s, kind], device(chip, 1 - core)).wait_recv()

    def sent(n):
        item = item_of(n)
        count = item // 32 % 4 + 1 - item // 16 % 2
        for times in range(1, degree + 2):

            @pl.when(count == times)
            def _():
                bulk = k_ref.at[pl.ds(0, times * 2 * rows)]
                remote(bulk, bulk, n, pair_sem.at[0, 0], device(chip, 1 - core)).wait_send()

    for kind in range(2):
        for piece in range(PIECES):
            send_on(0, row[0], kind, piece)
        across(0, chip, kind).start()
    loads[2].wait()

    wide = 2 * rows
    tiles = total_rows // TILE

    def first(tile):
        at = pl.ds(tile * TILE, TILE)
        keys = pl.ds(pl.multiple_of(chip * wide, wide), wide)
        s = lax.dot_general(
            q_ref[at], k_ref[keys], (((1,), (1,)), ((), ())), preferred_element_type=jnp.float32
        )
        place = core * rows + (tile * TILE + lax.broadcasted_iota(jnp.int32, s.shape, 0)) // group
        s = jnp.where(lax.broadcasted_iota(jnp.int32, s.shape, 1) <= place, s, -1e30)
        top = jnp.max(s, axis=1, keepdims=True)
        p = jnp.exp2((s - top) * factor)
        m_ref[at] = jnp.broadcast_to(top, (TILE, 128))
        part = p[:, :128]
        for j in range(128, wide, 128):
            part += p[:, j : j + 128]
        l_ref[at] = part
        acc_ref[at] = jnp.dot(p.astype(jnp.bfloat16), v_ref[keys], preferred_element_type=jnp.float32)

    def absorb(tile, s_chip):
        at = pl.ds(tile * TILE, TILE)
        keys = pl.ds(pl.multiple_of(s_chip * wide, wide), wide)
        s = lax.dot_general(
            q_ref[at], k_ref[keys], (((1,), (1,)), ((), ())), preferred_element_type=jnp.float32
        )
        old = m_ref[at]
        top = jnp.maximum(old, jnp.max(s, axis=1, keepdims=True))
        shrink = jnp.exp2((old - top) * factor)
        m_ref[at] = top
        ps = []
        part = l_ref[at] * shrink
        for j in range(0, wide, 128):
            p = jnp.exp2((s[:, j : j + 128] - top) * factor)
            part += p
            ps.append(p.astype(jnp.bfloat16))
        l_ref[at] = part
        p = jnp.concatenate(ps, axis=1)
        acc_ref[at] = acc_ref[at] * shrink + jnp.dot(
            p, v_ref[keys], preferred_element_type=jnp.float32
        )

    paired(chip)
    for tile in range(tiles):
        first(tile)

    def half(i, s):
        for tile in range(i * tiles // HALVES, (i + 1) * tiles // HALVES):
            absorb(tile, s)

    def step(n, waiting):
        item = item_of(n)
        fresh = item // 16 % 2 == 0
        pl.when(n >= LATE)(functools.partial(sent, n - LATE))
        ready = jnp.logical_and(fresh, waiting >= 0)
        for kind in range(2):
            relay(n, item, kind)
            if HALVES == 2 or kind == 1:

                @pl.when(ready)
                def _():
                    if kind == HALVES % 2:
                        paired(waiting)
                    half(kind if HALVES == 2 else 0, waiting)

        return jnp.where(fresh, item % 16, waiting)

    waiting = lax.fori_loop(1, item_count, step, jnp.int32(-1))

    @pl.when(waiting >= 0)
    def _():
        paired(waiting)
        for i in range(HALVES):
            half(i, waiting)

    for tile in range(tiles):
        at = pl.ds(tile * TILE, TILE)
        total = jnp.sum(l_ref[at], axis=1, keepdims=True)
        o_ref[at] = (acc_ref[at] * (1.0 / total)).astype(o_ref.dtype)

    def finish(n, carry):
        sent(n)
        return carry

    lax.fori_loop(jnp.maximum(item_count - LATE, 0), item_count, finish, 0)


def attend(ctx, queries, keys, values):
    count, heads, width = queries.shape
    group = heads // keys.shape[1]
    rows = count * group
    q = queries.reshape(rows, width)
    k = keys.reshape(count, width)
    v = values.reshape(count, width)
    chips = ctx // 2
    longest = max(len(row) for row in TABLE)
    far = [item % 16 for row in TABLE for item in row if item // 16 % 2]
    slots = ctx + max(far, default=-1) + 1
    anywhere = pl.BlockSpec(memory_space=pltpu.HBM)
    out = pl.pallas_call(
        functools.partial(kernel, chips, group),
        out_shape=jax.ShapeDtypeStruct((rows, width), queries.dtype),
        in_specs=[anywhere] * 3,
        out_specs=pl.BlockSpec(memory_space=pltpu.VMEM),
        scratch_shapes=[
            pltpu.VMEM((rows, width), queries.dtype),
            pltpu.VMEM((slots * count, width), keys.dtype),
            pltpu.VMEM((slots * count, width), values.dtype),
            pltpu.VMEM((rows, 128), jnp.float32),
            pltpu.VMEM((rows, 128), jnp.float32),
            pltpu.VMEM((rows, width), jnp.float32),
            pltpu.SemaphoreType.DMA((3,)),
            pltpu.SemaphoreType.DMA((slots - chips, 2, PIECES)),
            pltpu.SemaphoreType.DMA((chips, 2)),
            pltpu.SemaphoreType.DMA((longest,)),
        ],
        compiler_params=pltpu.CompilerParams(
            collective_id=0, has_side_effects=True, vmem_limit_bytes=32 * 1024 * 1024
        ),
        name="attend",
    )(*(pltpu.with_memory_space_constraint(a, pltpu.HBM) for a in (q, k, v)))
    return out.reshape(count, heads, width)


def solution(mesh):
    spec = P(("seq", "ctx"), "head", None)
    return jax.shard_map(
        functools.partial(attend, mesh.shape["ctx"]),
        mesh=mesh,
        in_specs=(spec, spec, spec),
        out_specs=spec,
        check_vma=False,
    )
```
